256 devices in a mesh: row: 8 (over z_hi, y), col: 32 (over x, z_lo, core).
Axes of the slice: x: 4, y: 4, z: 8 (z_hi: 2, z_lo: 4; z = z_hi * 4 + z_lo), core: 2. Of those that a mesh axis runs over, the one named last changes fastest.
Arguments:
- query_latent: bfloat16 [1024, 73728], P('row', 'col'), may hold values from -48 to 48
- kv_latent: bfloat16 [6144, 576], P('col'), may hold values from -6 to 6
- index_query: bfloat16 [1024, 8192], P('row'), may hold values from -18 to 18
- index_key: bfloat16 [6144, 128], P('col'), may hold values from -6 to 6
- head_weight: float32 [1024, 64], P('row'), may hold values from 0.05 to 0.5
- chosen: int32 [1024, 96], P('row'), may hold values from 0 to 1, as said below
- loss_grad: float32 [1024], P('row'), may hold values from 200 to 2000
Outputs:
- grad_query: float32 [1024, 8192], P('row', 'col')
- grad_key: float32 [6144, 128], P('col')
- grad_weight: float32 [1024, 64], P('row', 'col')
The draws below stay inside these ranges and needn't reach their ends.
Inputs may be any that keep to these rules, and one draw needn't show every extreme that they name: `chosen`: each query t has exactly 32 ones, all in blocks at or before the block that holds its position 5120 + t, and that block is always among them.
All inputs are finite; a program needn't handle non-finite values.
Results may differ from the reference program's by a relative error of at most 0.0033.
Values may be sent and summed in bfloat16 or wider, within the bound.
No kernel may reach another device: no remote copies, remote signals or barrier semaphores. Data moves between devices by JAX's collectives and lax.ppermute only.
A program may use at most 64 MiB of HBM per device.

```python
import math
import jax
import jax.numpy as jnp
from jax import lax

HEADS = 128
LATENT = 576
IDX_HEADS = 64
IDX_DIM = 128
BLOCK = 64
SELECT = 32
QUERIES = 1024
KEYS = 6144
NBLOCKS = 96


def clipped_normal(key, shape):
    return jnp.clip(jax.random.normal(key, shape, jnp.float32), -6.0, 6.0)


def drawn_keys(key, salt, width):
    return clipped_normal(jax.random.fold_in(key, salt), (KEYS, width))


def draw_kv_latent(key, part):
    return drawn_keys(key, 101, LATENT).astype(jnp.bfloat16)


def draw_query_latent(key, part):
    rows = clipped_normal(jax.random.fold_in(key, 103), (QUERIES, HEADS, LATENT))
    return rows.reshape(QUERIES, HEADS * LATENT).astype(jnp.bfloat16)


def draw_index_key(key, part):
    return drawn_keys(key, 201, IDX_DIM).astype(jnp.bfloat16)


def draw_index_query(key, part):
    rows = clipped_normal(jax.random.fold_in(key, 203), (QUERIES, IDX_HEADS, IDX_DIM))
    return rows.reshape(QUERIES, IDX_HEADS * IDX_DIM).astype(jnp.bfloat16)


def draw_chosen(key, part):
    query_pos = jnp.arange(QUERIES, dtype=jnp.int32) + (KEYS - QUERIES)
    own_block = query_pos // BLOCK
    blocks = jnp.arange(NBLOCKS, dtype=jnp.int32)
    raw = jax.random.randint(jax.random.fold_in(key, 301), (QUERIES, NBLOCKS), 0, 1 << 16)
    ranking = raw * NBLOCKS + blocks[None, :]
    ranking = jnp.where(blocks[None, :] <= own_block[:, None], ranking, -1)
    ranking = jnp.where(blocks[None, :] == own_block[:, None], (1 << 16) * NBLOCKS, ranking)
    values, indices = lax.top_k(ranking, SELECT)
    return jnp.sum((indices[:, :, None] == blocks[None, None, :]).astype(jnp.int32), axis=1)


def steps_of(stream_key, extent, cuts, low, top_value):
    factor_of, own = 1.0, jax.random.fold_in(stream_key, 6)
    for dim, shards_of in cuts:
        steps = jnp.exp(jax.random.uniform(jax.random.fold_in(own, dim), (shards_of,), jnp.float32, low / len(cuts), top_value / len(cuts)))
        factor_of = factor_of * jnp.repeat(steps, extent[dim] // shards_of).reshape([-1 if axis == dim else 1 for axis in range(len(extent))])
    return factor_of


def setup_inputs(seed: int = 0) -> dict:
    splits = jax.random.split(jax.random.key(seed), 8)
    return {
        "query_latent": draw_query_latent(jax.random.fold_in(splits[7], 71), 0),
        "kv_latent": draw_kv_latent(jax.random.fold_in(splits[7], 71), 0),
        "index_query": draw_index_query(jax.random.fold_in(splits[7], 71), 0),
        "index_key": draw_index_key(jax.random.fold_in(splits[7], 71), 0),
        "head_weight": jnp.clip(jnp.exp(math.log(0.5) - 2.3025851 * jax.random.uniform(splits[4], (QUERIES, IDX_HEADS), jnp.float32) ** steps_of(splits[4], (QUERIES, IDX_HEADS), ((0, 8),), -0.2, 0.2)), 0.05, 0.5),
        "chosen": draw_chosen(jax.random.fold_in(splits[7], 71), 0),
        "loss_grad": jnp.clip(jnp.exp(math.log(2000.0) - 2.3025851 * jax.random.uniform(splits[6], (QUERIES,), jnp.float32) ** steps_of(splits[6], (QUERIES,), ((0, 8),), -0.2, 0.2)), 200.0, 2000.0),
    }


mla_scale = 192.0 ** -0.5


def allowed_mask(chosen):
    expand = jnp.broadcast_to(chosen[:, :, None], (QUERIES, NBLOCKS, BLOCK)).reshape(QUERIES, KEYS)
    query_pos = jnp.arange(QUERIES, dtype=jnp.int32) + (KEYS - QUERIES)
    key_pos = jnp.arange(KEYS, dtype=jnp.int32)
    return (key_pos[None, :] <= query_pos[:, None]) & (expand > 0)


def reference(query_latent, kv_latent, index_query, index_key, head_weight, chosen, loss_grad):
    allowed = allowed_mask(chosen)
    per_head = query_latent.reshape(QUERIES, HEADS, LATENT).transpose(1, 0, 2)
    keys_turned = kv_latent.T

    def head_step(running, queries):
        scores = jnp.dot(queries, keys_turned, preferred_element_type=jnp.float32) * mla_scale
        masked = jnp.where(allowed, scores, -jnp.inf)
        highest = jnp.max(masked, axis=1, keepdims=True)
        raised = jnp.where(allowed, jnp.exp(masked - highest), 0.0)
        return running + raised / jnp.sum(raised, axis=1, keepdims=True), None

    summed, ignored = lax.scan(head_step, jnp.zeros((QUERIES, KEYS), jnp.float32), per_head)
    target = summed / HEADS
    inverse = IDX_DIM ** -0.5
    query_block = math.gcd(QUERIES, 64)
    block_count = QUERIES // query_block
    wide_keys = index_key.astype(jnp.float32)

    def index_block(inputs):
        index_rows, weights, cotangent, target_rows, allowed_rows = inputs
        rows_wide = index_rows.reshape(query_block, IDX_HEADS, IDX_DIM).astype(jnp.float32)
        affinity = jnp.einsum("tjd,sd->tjs", rows_wide, wide_keys) * inverse
        logits = jnp.sum(weights[:, :, None] * jax.nn.softplus(affinity), axis=1)
        masked = jnp.where(allowed_rows, logits, -jnp.inf)
        highest = jnp.max(masked, axis=1, keepdims=True)
        raised = jnp.where(allowed_rows, jnp.exp(masked - highest), 0.0)
        chance = raised / jnp.sum(raised, axis=1, keepdims=True)
        grad_logit = jnp.where(allowed_rows, cotangent[:, None] * (chance - target_rows), 0.0).astype(jnp.bfloat16)
        grad_wide = lax.optimization_barrier(grad_logit).astype(jnp.float32)
        slopes = (grad_wide[:, None, :] * jax.nn.sigmoid(affinity)).astype(jnp.bfloat16)
        slopes = lax.optimization_barrier(slopes).astype(jnp.float32)
        query_sum = jnp.einsum("tjs,sd->tjd", slopes, wide_keys)
        query_grads = (query_sum * (weights * inverse)[:, :, None]).reshape(query_block, IDX_HEADS * IDX_DIM)
        weighted = (weights[:, :, None] * rows_wide).astype(jnp.bfloat16)
        weighted = lax.optimization_barrier(weighted).astype(jnp.float32)
        key_part = jnp.einsum("tjs,tjd->sd", slopes, weighted)
        weight_grads = jnp.sum(grad_wide[:, None, :] * jax.nn.softplus(affinity), axis=2)
        return query_grads, weight_grads, key_part

    stacked = (index_query.reshape(block_count, query_block, IDX_HEADS * IDX_DIM),
               head_weight.reshape(block_count, query_block, IDX_HEADS),
               loss_grad.reshape(block_count, query_block),
               target.reshape(block_count, query_block, KEYS),
               allowed.reshape(block_count, query_block, KEYS))
    query_grads, weight_grads, key_parts = lax.map(index_block, stacked)
    grad_query = query_grads.reshape(QUERIES, IDX_HEADS * IDX_DIM)
    grad_weight = weight_grads.reshape(QUERIES, IDX_HEADS)
    grad_key = jnp.sum(key_parts, axis=0) * inverse
    return grad_query, grad_key, grad_weight
```

```python
import jax
import jax.numpy as jnp
from jax import lax
from jax.experimental import pallas as pl
from jax.experimental.pallas import tpu as pltpu
from jax.sharding import Mesh, PartitionSpec as P

LATENT = 576
IDX_DIM = 128
IDX_HEADS = 64
HEADS = 128
BLOCK = 64
SELECT = 32
MINE = 4
KEYS = 6144
HALF = KEYS // 2
SEL_KEYS = SELECT * BLOCK
WIDE = IDX_DIM + LATENT
mla_scale = 192.0 ** (-0.5)
inverse = IDX_DIM ** (-0.5)
big_negative = -1e30
COL = ("x", "zl", "core")
Z = ("zh", "zl")

PIECES = (512, 512, 256, 256, 512, 256, 256, 128, 128, 256)


def shift(value, axis, size, by):
    return lax.ppermute(value, axis, [(i, (i + by) % size) for i in range(size)])


def gather_keys(index_key, kv_latent):
    own = jnp.concatenate([index_key, kv_latent], axis=1)
    a, b = own[:128], own[128:]
    za1, za3 = shift(a, Z, 8, -1), shift(a, Z, 8, 1)
    za2l, za2h = shift(a[:64], Z, 8, 2), shift(a[64:], Z, 8, -2)
    xb1, xb3 = shift(b, "x", 4, -1), shift(b, "x", 4, 1)
    xb2l, xb2h = shift(xb1[:32], "x", 4, -1), shift(xb3[32:], "x", 4, 1)
    ua = jnp.concatenate([a, za1, za2l, za2h, za3], axis=0)
    ub = jnp.concatenate([b, xb1, xb2l, xb2h, xb3], axis=0)
    xa1, xa3 = shift(ua, "x", 4, -1), shift(ua, "x", 4, 1)
    xa2l, xa2h = shift(xa1[:256], "x", 4, -1), shift(xa3[256:], "x", 4, 1)
    zb1, zb3 = shift(ub, Z, 8, -1), shift(ub, Z, 8, 1)
    zb2l, zb2h = shift(ub[:128], Z, 8, 2), shift(ub[128:], Z, 8, -2)
    mine = [ua, xa1, xa2l, xa2h, xa3, ub, zb1, zb2l, zb2h, zb3]
    return mine + [shift(piece, "core", 2, 1) for piece in mine]


def last(a, b):
    return lax.dot_general(a, b, (((1,), (1,)), ((), ())), preferred_element_type=jnp.float32)


def kernel(kpos, gpos, upto, cot, queries, iq, wide_w, *rest):
    pieces = rest[:20]
    out, gk0, gk1 = rest[20:23]
    kbuf, ksel, gacc, outs, sems = rest[23:]
    copies = []
    start = 0
    for n in range(20):
        rows = PIECES[n % 10]
        copies.append(pltpu.make_async_copy(pieces[n], kbuf.at[pl.ds(start, rows)], sems.at[n]))
        start += rows
    for copy in copies:
        copy.start()
    gacc[...] = jnp.zeros_like(gacc)
    for copy in copies:
        copy.wait()
    lane = lax.broadcasted_iota(jnp.int32, (1, SEL_KEYS), 1)
    for q in range(MINE):
        for k in range(SELECT):
            at = pl.multiple_of(kpos[q * SELECT + k], BLOCK)
            ksel[k * BLOCK : (k + 1) * BLOCK, :] = kbuf[pl.ds(at, BLOCK), :]
        pick = (
            lax.broadcasted_iota(jnp.int32, (32, 128), 1)
            == lax.broadcasted_iota(jnp.int32, (32, 128), 0) * MINE + q
        )
        rows = jnp.dot(
            pick.astype(jnp.bfloat16), queries[...], preferred_element_type=jnp.float32
        ).astype(jnp.bfloat16)
        heads = jnp.concatenate([rows[:, h * LATENT : (h + 1) * LATENT] for h in range(4)], axis=0)
        valid = lane <= upto[q] + (SEL_KEYS - BLOCK)
        scores = jnp.where(valid, last(heads, ksel[:, IDX_DIM:]) * mla_scale, big_negative)
        raised = jnp.exp(scores - jnp.max(scores, axis=1, keepdims=True))
        part = 1.0 / jnp.sum(raised, axis=1, keepdims=True)
        target = jnp.sum(raised * part, axis=0, keepdims=True) * (1.0 / HEADS)
        iq_rows = iq[q * IDX_HEADS : (q + 1) * IDX_HEADS, :]
        weight = wide_w[q * IDX_HEADS : (q + 1) * IDX_HEADS, :]
        w1 = weight[:, :1]
        affinity = last(iq_rows, ksel[:, :IDX_DIM]) * inverse
        small = jnp.exp(-jnp.abs(affinity))
        soft = jnp.maximum(affinity, 0.0) + jnp.log(1.0 + small)
        gate = jnp.where(affinity >= 0.0, 1.0, small) / (1.0 + small)
        logits = jnp.where(valid, jnp.sum(w1 * soft, axis=0, keepdims=True), big_negative)
        up = jnp.exp(logits - jnp.max(logits, axis=1, keepdims=True))
        chance = up / jnp.sum(up, axis=1, keepdims=True)
        grad_logit = jnp.where(valid, cot[q] * (chance - target), 0.0)
        grad_wide = grad_logit.astype(jnp.bfloat16).astype(jnp.float32)
        slopes = (grad_wide * gate).astype(jnp.bfloat16)
        weighted = (weight * iq_rows.astype(jnp.float32)).astype(jnp.bfloat16)
        gq = jnp.dot(slopes, ksel[:, :IDX_DIM], preferred_element_type=jnp.float32)
        gq = gq * (weight * inverse)
        gw = jnp.sum(grad_wide * soft, axis=1, keepdims=True)
        outs[:, 2 * q : 2 * q + 2, :] = gq.reshape(32, 2, 128)
        outs[:, 8 + 2 * q : 10 + 2 * q, :] = jnp.broadcast_to(gw, (64, 128)).reshape(32, 2, 128)
        gk = lax.dot_general(
            slopes, weighted, (((0,), (0,)), ((), ())), preferred_element_type=jnp.float32
        )
        for k in range(SELECT):
            at = pl.multiple_of(gpos[q * SELECT + k], BLOCK)
            gacc[pl.ds(at, BLOCK), :] += gk[k * BLOCK : (k + 1) * BLOCK, :]
    out[...] = outs[...].astype(jnp.bfloat16)
    gk0[...] = gacc[:HALF, :]
    gk1[...] = gacc[HALF:, :].astype(jnp.bfloat16)


def body(query_latent, kv_latent, index_query, index_key, head_weight, chosen, loss_grad):
    x, zl, core = lax.axis_index("x"), lax.axis_index("zl"), lax.axis_index("core")
    col = (x * 4 + zl) * 2 + core
    pieces = gather_keys(index_key, kv_latent)
    queries = lax.all_to_all(query_latent, COL, 0, 0, tiled=True)
    first = col * MINE
    picked = lax.dynamic_slice_in_dim(chosen, first, MINE, 0)
    nblocks = picked.shape[1]
    before = jnp.tril(jnp.ones((nblocks, nblocks), jnp.int32), -1)
    rank = jnp.sum(picked[:, None, :] * before[None], axis=2)
    hit = (rank[:, :, None] == jnp.arange(SELECT)[None, None, :]) & (picked[:, :, None] > 0)
    block = jnp.sum(jnp.where(hit, jnp.arange(nblocks)[None, :, None], 0), axis=1)
    owner, sub = block // 3, block % 3
    dx, dz, dc = (owner // 8 - x) % 4, (owner // 2 % 4 - zl) % 4, (owner + core) % 2
    kpos = dc * HALF + jnp.where(
        sub < 2, dx * 512 + dz * 128 + sub * BLOCK, 2048 + dz * 256 + dx * BLOCK
    )
    gpos = ((dc * 4 + dx) * 4 + dz) * 192 + sub * BLOCK
    row = lax.axis_index("zh") * 4 + lax.axis_index("y")
    upto = (KEYS - 1024 + row * 128 + first + jnp.arange(MINE)) % BLOCK
    cot = lax.dynamic_slice_in_dim(loss_grad, first, MINE, 0)
    iq = lax.dynamic_slice_in_dim(index_query, first, MINE, 0).reshape(MINE * IDX_HEADS, IDX_DIM)
    weight = lax.dynamic_slice_in_dim(head_weight, first, MINE, 0).reshape(MINE * IDX_HEADS, 1)
    weight = jnp.broadcast_to(weight, (MINE * IDX_HEADS, 128))
    smem = pl.BlockSpec(memory_space=pltpu.SMEM)
    vmem = pl.BlockSpec(memory_space=pltpu.VMEM)
    out, gk0, gk1 = pl.pallas_call(
        kernel,
        out_shape=(
            jax.ShapeDtypeStruct((32, 16, 128), jnp.bfloat16),
            jax.ShapeDtypeStruct((HALF, 128), jnp.float32),
            jax.ShapeDtypeStruct((HALF, 128), jnp.bfloat16),
        ),
        in_specs=[smem] * 4 + [vmem] * 3 + [pl.BlockSpec(memory_space=pl.ANY)] * 20,
        out_specs=(vmem, vmem, vmem),
        scratch_shapes=[
            pltpu.VMEM((KEYS, WIDE), jnp.bfloat16),
            pltpu.VMEM((SEL_KEYS, WIDE), jnp.bfloat16),
            pltpu.VMEM((KEYS, 128), jnp.float32),
            pltpu.VMEM((32, 16, 128), jnp.float32),
            pltpu.SemaphoreType.DMA((20,)),
        ],
        cost_estimate=pl.CostEstimate(
            flops=2 * MINE * SEL_KEYS * (HEADS * LATENT + 3 * IDX_HEADS * IDX_DIM),
            bytes_accessed=KEYS * WIDE * 2,
            transcendentals=MINE * SEL_KEYS * 256,
        ),
    )(kpos.reshape(-1), gpos.reshape(-1), upto, cot, queries, iq, weight, *pieces)

    part = (gk0 + shift(gk1, "core", 2, 1).astype(jnp.float32)).reshape(4, 768, 128)
    low = part.astype(jnp.bfloat16)
    part = (
        part[0]
        + shift(low[1], "x", 4, 1)
        + shift(low[2], "x", 4, 2)
        + shift(low[3], "x", 4, -1)
    ).reshape(4, 192, 128)
    part = part[0] + shift(part[1], Z, 8, 1) + shift(part[2], Z, 8, 2) + shift(part[3], Z, 8, -1)
    part = part + shift(part, "zh", 2, 1)
    part = (part + shift(part, "y", 4, 2)) + (shift(part, "y", 4, 1) + shift(part, "y", 4, -1))
    grad_key = part * inverse

    back = lax.all_to_all(out, COL, 0, 0, tiled=True).astype(jnp.float32)
    grad_query = back[:, :8, :].reshape(128, 256)
    grad_weight = back[:, 8:, 0].reshape(128, 2)
    return grad_query, grad_key, grad_weight


def solution(mesh):
    wide = Mesh(mesh.devices.reshape(2, 4, 4, 4, 2), ("zh", "y", "x", "zl", "core"))
    row = ("zh", "y")
    in_specs = (
        P(row, COL),
        P(COL, None),
        P(row, None),
        P(COL, None),
        P(row, None),
        P(row, None),
        P(row),
    )
    out_specs = (P(row, COL), P(COL, None), P(row, COL))
    return jax.shard_map(body, mesh=wide, in_specs=in_specs, out_specs=out_specs, check_vma=False)
```

```python
import jax
import jax.numpy as jnp
from jax import lax
from jax.experimental import pallas as pl
from jax.experimental.pallas import tpu as pltpu
from jax.sharding import Mesh, PartitionSpec as P

LATENT = 576
IDX_DIM = 128
IDX_HEADS = 64
HEADS = 128
BLOCK = 64
HALF = BLOCK // 2
SELECT = 32
MINE = 4
KEYS = 6144
SEL_KEYS = SELECT * BLOCK
MID = SEL_KEYS // 2
ROWS_A = 160
ROWS_B = 192
A, B = 3 * ROWS_A, 3 * ROWS_B
mla_scale = 192.0 ** (-0.5)
inverse = IDX_DIM ** (-0.5)
big_negative = -1e30
COL = ("x", "zl", "core")
Z = ("zh", "zl")
bf16, f32 = jnp.bfloat16, jnp.float32
SMEM = pl.BlockSpec(memory_space=pltpu.SMEM)
VMEM = pl.BlockSpec(memory_space=pltpu.VMEM)
ANY = pl.BlockSpec(memory_space=pl.ANY)


def struct(shape, dtype):
    return jax.ShapeDtypeStruct(shape, dtype)


def call(kernel, ins, out_shape, flops=0, nbytes=1 << 20, scratch=(), specs=None):
    return pl.pallas_call(
        kernel,
        out_shape=out_shape,
        in_specs=specs or [VMEM] * len(ins),
        out_specs=jax.tree.map(lambda _: VMEM, out_shape),
        scratch_shapes=scratch,
        cost_estimate=pl.CostEstimate(flops=flops, bytes_accessed=nbytes, transcendentals=0),
    )(*ins)


def shift(value, axis, size, by):
    return lax.ppermute(value, axis, [(i, (i + by) % size) for i in range(size)])


def around_z(value):
    two = [(2 * z + c, 2 * ((z + (2, -2)[c]) % 8) + c) for z in range(8) for c in range(2)]
    return [
        shift(value, Z, 8, -1),
        lax.ppermute(value, ("zh", "zl", "core"), two),
        shift(value, Z, 8, 1),
    ]


def around_x(value):
    return [shift(value, "x", 4, -1), shift(value, "x", 4, 2), shift(value, "x", 4, 1)]


def pack_kernel(ik, kv, a, b):
    for s in range(3):
        at = slice(s * BLOCK, (s + 1) * BLOCK)
        low, high = s * BLOCK, s * BLOCK + HALF
        a[s * ROWS_A : s * ROWS_A + 64, :] = kv[at, 0:128]
        a[s * ROWS_A + 64 : s * ROWS_A + 128, :] = kv[at, 128:256]
        a[s * ROWS_A + 128 : (s + 1) * ROWS_A, :] = jnp.concatenate(
            [kv[low:high, 512:576], kv[high : high + HALF, 512:576]], axis=1
        )
        b[s * ROWS_B : s * ROWS_B + 64, :] = kv[at, 256:384]
        b[s * ROWS_B + 64 : s * ROWS_B + 128, :] = kv[at, 384:512]
        b[s * ROWS_B + 128 : (s + 1) * ROWS_B, :] = ik[at, :]


def join_kernel(*refs):
    out = refs[-1]
    start = 0
    for ref in refs[:-1]:
        out[start : start + ref.shape[0], :] = ref[...]
        start += ref.shape[0]


def join(parts):
    rows = sum(part.shape[0] for part in parts)
    return call(join_kernel, parts, struct((rows, 128), bf16))


def gather_keys(index_key, kv_latent):
    a, b = call(
        pack_kernel, (index_key, kv_latent), (struct((A, 128), bf16), struct((B, 128), bf16))
    )
    ua = join([a] + around_z(a))
    ub = join([b] + around_x(b))
    mine = [ua] + around_x(ua) + [ub] + around_z(ub)
    other = [shift(piece, "core", 2, 1) for piece in mine]
    return mine[:4] + other[:4] + mine[4:] + other[4:]


def last(a, b):
    return lax.dot_general(a, b, (((1,), (1,)), ((), ())), preferred_element_type=f32)


def query_kernel(queries, wide, rope):
    zero = jnp.zeros((HEADS, 64), bf16)
    for q in range(MINE):
        pick = (
            lax.broadcasted_iota(jnp.int32, (32, 128), 1)
            == lax.broadcasted_iota(jnp.int32, (32, 128), 0) * MINE + q
        )
        rows = jnp.dot(pick.astype(bf16), queries[...], preferred_element_type=f32).astype(bf16)
        heads = jnp.concatenate([rows[:, h * LATENT : (h + 1) * LATENT] for h in range(4)], axis=0)
        wide[q * HEADS : (q + 1) * HEADS, :] = heads[:, :512]
        rope[q * 256 : q * 256 + 128, :] = jnp.concatenate([heads[:, 512:], zero], axis=1)
        rope[q * 256 + 128 : (q + 1) * 256, :] = jnp.concatenate([zero, heads[:, 512:]], axis=1)


def kernel(apos, bpos, gpos, dest, upto, cot, wide, rope, iq, wide_w, *rest):
    pieces = rest[:16]
    away, gk0, gq0 = rest[16:19]
    abuf, bbuf, ksel, rsel, isel, gacc, outs, sems = rest[19:]
    copies = []
    for n in range(16):
        buf, rows = (abuf, 4 * A) if n < 8 else (bbuf, 4 * B)
        copies.append(
            pltpu.make_async_copy(pieces[n], buf.at[pl.ds(n % 8 * rows, rows)], sems.at[n])
        )
    for copy in copies:
        copy.start()
    gacc[...] = jnp.zeros_like(gacc)
    for copy in copies:
        copy.wait()
    lane = lax.broadcasted_iota(jnp.int32, (1, SEL_KEYS), 1)
    place = jnp.where(lane < MID, lane - (MID - HALF), lane - (SEL_KEYS - HALF) + HALF)
    place = jnp.where((lane >= MID) & (lane < SEL_KEYS - HALF), -1, place)
    for q in range(MINE):
        for k in range(SELECT):
            at = pl.multiple_of(apos[q * SELECT + k], 32)
            bt = pl.multiple_of(bpos[q * SELECT + k], 64)
            for h in range(2):
                to = slice(h * MID + k * HALF, h * MID + (k + 1) * HALF)
                off = h * HALF
                ksel[to, 0:128] = abuf[pl.ds(at + off, HALF), :]
                ksel[to, 128:256] = abuf[pl.ds(at + 64 + off, HALF), :]
                ksel[to, 256:384] = bbuf[pl.ds(bt + off, HALF), :]
                ksel[to, 384:512] = bbuf[pl.ds(bt + 64 + off, HALF), :]
                isel[to, :] = bbuf[pl.ds(bt + 128 + off, HALF), :]
            rsel[k * HALF : (k + 1) * HALF, :] = abuf[pl.ds(at + 128, HALF), :]
        valid = place <= upto[q]
        turned = last(rope[q * 256 : (q + 1) * 256, :], rsel[...])
        scores = last(wide[q * HEADS : (q + 1) * HEADS, :], ksel[...]) + jnp.concatenate(
            [turned[:HEADS], turned[HEADS:]], axis=1
        )
        scores = jnp.where(valid, scores * mla_scale, big_negative)
        raised = jnp.exp(scores - jnp.max(scores, axis=1, keepdims=True))
        part = 1.0 / jnp.sum(raised, axis=1, keepdims=True)
        target = jnp.sum(raised * part, axis=0, keepdims=True) * (1.0 / HEADS)
        iq_rows = iq[q * IDX_HEADS : (q + 1) * IDX_HEADS, :]
        weight = wide_w[q * IDX_HEADS : (q + 1) * IDX_HEADS, :]
        affinity = last(iq_rows, isel[...]) * inverse
        small = jnp.exp(-jnp.abs(affinity))
        soft = jnp.maximum(affinity, 0.0) + jnp.log(1.0 + small)
        gate = jnp.where(affinity >= 0.0, 1.0, small) / (1.0 + small)
        logits = jnp.where(valid, jnp.sum(weight[:, :1] * soft, axis=0, keepdims=True), big_negative)
        up = jnp.exp(logits - jnp.max(logits, axis=1, keepdims=True))
        chance = up / jnp.sum(up, axis=1, keepdims=True)
        grad_logit = jnp.where(valid, cot[q] * (chance - target), 0.0)
        grad_wide = grad_logit.astype(bf16).astype(f32)
        slopes = (grad_wide * gate).astype(bf16)
        weighted = (weight * iq_rows.astype(f32)).astype(bf16)
        gq = jnp.dot(slopes, isel[...], preferred_element_type=f32) * (weight * inverse)
        gw = jnp.sum(grad_wide * soft, axis=1, keepdims=True)
        outs[:, 2 * q : 2 * q + 2, :] = gq.reshape(32, 2, 128)
        outs[:, 8 + 2 * q : 10 + 2 * q, :] = jnp.broadcast_to(gw, (64, 128)).reshape(32, 2, 128)
        gk = lax.dot_general(slopes, weighted, (((0,), (0,)), ((), ())), preferred_element_type=f32)
        for k in range(SELECT):
            at = pl.multiple_of(gpos[q * SELECT + k], BLOCK)
            gacc[pl.ds(at, HALF), :] += gk[k * HALF : (k + 1) * HALF, :]
            gacc[pl.ds(at + HALF, HALF), :] += gk[MID + k * HALF : MID + (k + 1) * HALF, :]
    gk0[...] = gacc[: KEYS // 2, :]
    away[: KEYS // 2, :] = gacc[KEYS // 2 :, :].astype(bf16)
    for n in range(16):
        gq0[n * 16 : (n + 1) * 16, :] = outs[dest[n]].astype(bf16)
        away[KEYS // 2 + n * 16 : KEYS // 2 + (n + 1) * 16, :] = outs[dest[16 + n]].astype(bf16)


def x_kernel(gk0, gq0, got, own, own_q, m1, m2, m3):
    for dx in range(4):
        at = slice(dx * 768, (dx + 1) * 768)
        total = gk0[at, :] + got[at, :].astype(f32)
        mine = gq0[dx * 64 : (dx + 1) * 64, :]
        others = got[3072 + dx * 64 : 3072 + (dx + 1) * 64, :]
        if dx == 0:
            own[...] = total
            own_q[:64, :] = mine
            own_q[64:, :] = others
        else:
            m = (m1, m2, m3)[dx - 1]
            m[:768, :] = total.astype(bf16)
            m[768:832, :] = mine
            m[832:, :] = others


def z_kernel(own, own_q, r1, r2, r3, out, out_q, m1, m2, m3):
    total = own[...]
    for r in (r1, r2, r3):
        total = total + r[:768, :].astype(f32)
    for dz in range(4):
        part = total[dz * 192 : (dz + 1) * 192]
        if dz == 0:
            out[...] = part
            to, base = out_q, 0
        else:
            to, base = (m1, m2, m3)[dz - 1], 192
            to[:192, :] = part.astype(bf16)
        for sx in range(4):
            src, off = (own_q, 0) if sx == 0 else ((r1, r2, r3)[sx - 1], 768)
            for sc in range(2):
                at = base + (sx * 2 + sc) * 16
                to[at : at + 16, :] = src[off + sc * 64 + dz * 16 : off + sc * 64 + dz * 16 + 16, :]


def end_kernel(source, own, own_q, r1, r2, r3, out, gq, gw):
    total = own[...]
    for r in (r1, r2, r3):
        total = total + r[:192, :].astype(f32)
    out[...] = total
    for sz in range(4):
        src, off = (own_q, 0) if sz == 0 else ((r1, r2, r3)[sz - 1], 192)
        for n in range(8):
            block = src[off + n * 16 : off + (n + 1) * 16, :].astype(f32)
            at = source[sz * 8 + n]
            gq[at] = block[:8]
            gw[at] = block[8:]


def body(query_latent, kv_latent, index_query, index_key, head_weight, chosen, loss_grad):
    x, zl, core = lax.axis_index("x"), lax.axis_index("zl"), lax.axis_index("core")
    col = (x * 4 + zl) * 2 + core
    pieces = gather_keys(index_key, kv_latent)
    queries = lax.all_to_all(query_latent, COL, 0, 0, tiled=True)
    wide, rope = call(
        query_kernel, (queries,), (struct((512, 512), bf16), struct((1024, 128), bf16))
    )
    first = col * MINE
    picked = lax.dynamic_slice_in_dim(chosen, first, MINE, 0)
    nblocks = picked.shape[1]
    before = jnp.tril(jnp.ones((nblocks, nblocks), jnp.int32), -1)
    rank = jnp.sum(picked[:, None, :] * before[None], axis=2)
    hit = (rank[:, :, None] == jnp.arange(SELECT)[None, None, :]) & (picked[:, :, None] > 0)
    block = jnp.sum(jnp.where(hit, jnp.arange(nblocks)[None, :, None], 0), axis=1).reshape(-1)
    owner, sub = block // 3, block % 3
    dx, dz, dc = (owner // 8 - x) % 4, (owner // 2 % 4 - zl) % 4, (owner + core) % 2
    apos = ((dc * 4 + dx) * 4 + dz) * A + sub * ROWS_A
    bpos = ((dc * 4 + dz) * 4 + dx) * B + sub * ROWS_B
    gpos = ((dc * 4 + dx) * 4 + dz) * 192 + sub * BLOCK
    row = lax.axis_index("zh") * 4 + lax.axis_index("y")
    upto = (KEYS - 1024 + row * 128 + first + jnp.arange(MINE)) % BLOCK
    n = jnp.arange(32)
    dest = (((x + n // 4 % 4) % 4) * 4 + (zl + n % 4) % 4) * 2 + (core + n // 16) % 2
    source = (((x - n // 2 % 4) % 4) * 4 + (zl - n // 8) % 4) * 2 + (core + n % 2) % 2
    cot = lax.dynamic_slice_in_dim(loss_grad, first, MINE, 0)
    iq = lax.dynamic_slice_in_dim(index_query, first, MINE, 0).reshape(MINE * IDX_HEADS, IDX_DIM)
    weight = lax.dynamic_slice_in_dim(head_weight, first, MINE, 0).reshape(MINE * IDX_HEADS, 1)
    weight = jnp.broadcast_to(weight, (MINE * IDX_HEADS, 128))
    away, gk0, gq0 = call(
        kernel,
        (apos, bpos, gpos, dest, upto, cot, wide, rope, iq, weight, *pieces),
        (struct((3328, 128), bf16), struct((3072, 128), f32), struct((256, 128), bf16)),
        flops=2 * MINE * SEL_KEYS * (HEADS * LATENT + 3 * IDX_HEADS * IDX_DIM),
        nbytes=KEYS * 704 * 2,
        scratch=[
            pltpu.VMEM((32 * A, 128), bf16),
            pltpu.VMEM((32 * B, 128), bf16),
            pltpu.VMEM((SEL_KEYS, 512), bf16),
            pltpu.VMEM((MID, 128), bf16),
            pltpu.VMEM((SEL_KEYS, 128), bf16),
            pltpu.VMEM((KEYS, 128), f32),
            pltpu.VMEM((32, 16, 128), f32),
            pltpu.SemaphoreType.DMA((16,)),
        ],
        specs=[SMEM] * 6 + [VMEM] * 4 + [ANY] * 16,
    )

    got = shift(away, "core", 2, 1)
    message = struct((896, 128), bf16)
    own, own_q, *m = call(
        x_kernel,
        (gk0, gq0, got),
        (struct((768, 128), f32), struct((128, 128), bf16), message, message, message),
    )
    r = [shift(m[0], "x", 4, 1), shift(m[1], "x", 4, 2), shift(m[2], "x", 4, -1)]
    message = struct((320, 128), bf16)
    own, own_q, *m = call(
        z_kernel,
        (own, own_q, *r),
        (struct((192, 128), f32), struct((128, 128), bf16), message, message, message),
    )
    r = [shift(m[0], "zl", 4, 1), shift(m[1], "zl", 4, 2), shift(m[2], "zl", 4, -1)]
    part, gq, gw = call(
        end_kernel,
        (source, own, own_q, *r),
        (struct((192, 128), f32), struct((32, 8, 128), f32), struct((32, 8, 128), f32)),
        specs=[SMEM] + [VMEM] * 5,
    )
    part = part + shift(part, "zh", 2, 1)
    part = (part + shift(part, "y", 4, 2)) + (shift(part, "y", 4, 1) + shift(part, "y", 4, -1))
    return gq.reshape(128, 256), part * inverse, gw[:, :, 0].reshape(128, 2)


def solution(mesh):
    wide = Mesh(mesh.devices.reshape(2, 4, 4, 4, 2), ("zh", "y", "x", "zl", "core"))
    row = ("zh", "y")
    in_specs = (
        P(row, COL),
        P(COL, None),
        P(row, None),
        P(COL, None),
        P(row, None),
        P(row, None),
        P(row),
    )
    out_specs = (P(row, COL), P(COL, None), P(row, COL))
    return jax.shard_map(body, mesh=wide, in_specs=in_specs, out_specs=out_specs, check_vma=False)
```

```python
import jax
import jax.numpy as jnp
from jax import lax
from jax.experimental import pallas as pl
from jax.experimental.pallas import tpu as pltpu
from jax.sharding import Mesh, PartitionSpec as P

LATENT = 576
IDX_DIM = 128
IDX_HEADS = 64
HEADS = 128
BLOCK = 64
HALF = BLOCK // 2
SELECT = 32
MINE = 4
KEYS = 6144
SEL_KEYS = SELECT * BLOCK
MID = SEL_KEYS // 2
ROWS_A = 160
ROWS_B = 192
A, B = 3 * ROWS_A, 3 * ROWS_B
mla_scale = 192.0 ** (-0.5)
inverse = IDX_DIM ** (-0.5)
log2e = 1.4426950408889634
big_negative = -1e30
COL = ("x", "zl", "core")
Z = ("zh", "zl")
bf16, f32 = jnp.bfloat16, jnp.float32
SMEM = pl.BlockSpec(memory_space=pltpu.SMEM)
VMEM = pl.BlockSpec(memory_space=pltpu.VMEM)
ANY = pl.BlockSpec(memory_space=pl.ANY)


def struct(shape, dtype):
    return jax.ShapeDtypeStruct(shape, dtype)


def call(kernel, ins, out_shape, flops=0, nbytes=1 << 20, scratch=(), specs=None):
    return pl.pallas_call(
        kernel,
        out_shape=out_shape,
        in_specs=specs or [VMEM] * len(ins),
        out_specs=jax.tree.map(lambda _: VMEM, out_shape),
        scratch_shapes=scratch,
        cost_estimate=pl.CostEstimate(flops=flops, bytes_accessed=nbytes, transcendentals=0),
    )(*ins)


def shift(value, axis, size, by):
    return lax.ppermute(value, axis, [(i, (i + by) % size) for i in range(size)])


def around_z(value):
    two = [(2 * z + c, 2 * ((z + (2, -2)[c]) % 8) + c) for z in range(8) for c in range(2)]
    return [
        shift(value, Z, 8, -1),
        lax.ppermute(value, ("zh", "zl", "core"), two),
        shift(value, Z, 8, 1),
    ]


def around_x(value):
    return [shift(value, "x", 4, -1), shift(value, "x", 4, 2), shift(value, "x", 4, 1)]


def pack_kernel(ik, kv, a, b):
    for s in range(3):
        at = slice(s * BLOCK, (s + 1) * BLOCK)
        low, high = s * BLOCK, s * BLOCK + HALF
        a[s * ROWS_A : s * ROWS_A + 64, :] = kv[at, 0:128]
        a[s * ROWS_A + 64 : s * ROWS_A + 128, :] = kv[at, 128:256]
        a[s * ROWS_A + 128 : (s + 1) * ROWS_A, :] = jnp.concatenate(
            [kv[low:high, 512:576], kv[high : high + HALF, 512:576]], axis=1
        )
        b[s * ROWS_B : s * ROWS_B + 64, :] = kv[at, 256:384]
        b[s * ROWS_B + 64 : s * ROWS_B + 128, :] = kv[at, 384:512]
        b[s * ROWS_B + 128 : (s + 1) * ROWS_B, :] = ik[at, :]


def join_kernel(*refs):
    for n in range(8):
        rows = refs[n].shape[0]
        refs[8 + n // 4][n % 4 * rows : (n % 4 + 1) * rows, :] = refs[n][...]


def join(first, second):
    out = (struct((4 * A, 128), bf16), struct((4 * B, 128), bf16))
    return call(join_kernel, first + second, out)


def gather_keys(index_key, kv_latent, query_latent):
    a, b = call(
        pack_kernel, (index_key, kv_latent), (struct((A, 128), bf16), struct((B, 128), bf16))
    )
    near_z, near_x = around_z(a), around_x(b)
    near_z, near_x = lax.optimization_barrier((near_z, near_x))
    ua, ub = join([a] + near_z, [b] + near_x)
    queries = lax.all_to_all(query_latent, COL, 0, 0, tiled=True)
    return [ua] + around_x(ua) + [ub] + around_z(ub), queries


def last(a, b):
    return lax.dot_general(a, b, (((1,), (1,)), ((), ())), preferred_element_type=f32)


def query_kernel(queries, wide):
    zero = jnp.zeros((HEADS, 64), bf16)
    for q in range(MINE):
        pick = (
            lax.broadcasted_iota(jnp.int32, (32, 128), 1)
            == lax.broadcasted_iota(jnp.int32, (32, 128), 0) * MINE + q
        )
        rows = jnp.dot(pick.astype(bf16), queries[...], preferred_element_type=f32).astype(bf16)
        heads = jnp.concatenate([rows[:, h * LATENT : (h + 1) * LATENT] for h in range(4)], axis=0)
        wide[q * HEADS : (q + 1) * HEADS, :] = jnp.concatenate([heads, zero], axis=1)


def masked(values, valid):
    one, two = slice(MID - 128, MID), slice(SEL_KEYS - 128, SEL_KEYS)
    return jnp.concatenate(
        [
            values[:, : MID - 128],
            jnp.where(valid[:, one], values[:, one], big_negative),
            values[:, MID : SEL_KEYS - 128],
            jnp.where(valid[:, two], values[:, two], big_negative),
        ],
        axis=1,
    )


def gate_kernel(index_query, index_key, head_weight, gates, turned):
    lane = lax.broadcasted_iota(jnp.int32, head_weight.shape, 1)

    @pl.loop(0, IDX_HEADS)
    def _(j):
        rows = pl.ds(pl.multiple_of(j * 128, 128), 128)
        iq = index_query[:, rows]
        affinity = last(iq, index_key[...]) * inverse
        small = jnp.exp2(jnp.abs(affinity) * (-log2e))
        gate = jnp.where(affinity >= 0.0, 1.0, small) / (1.0 + small)
        gates[rows, :] = gate.astype(bf16)
        weight = jnp.sum(jnp.where(lane == j, head_weight[...], 0.0), axis=1, keepdims=True)
        turned[:, rows] = (weight * iq.astype(f32)).astype(bf16).T


def kernel(apos, bpos, upto, cot, wide, iq, wide_w, place_of, *rest):
    pieces = rest[:16]
    out = rest[16]
    abuf, bbuf, ksel, isel, scores, softs, gates, slopes, outs, sems = rest[17:]
    copies = []
    for n in range(16):
        buf, rows = (abuf, 4 * A) if n < 8 else (bbuf, 4 * B)
        copies.append(
            pltpu.make_async_copy(pieces[n], buf.at[pl.ds(n % 8 * rows, rows)], sems.at[n])
        )
    for copy in copies:
        copy.start()
    outs[...] = jnp.zeros_like(outs)
    for copy in copies:
        copy.wait()
    lane = lax.broadcasted_iota(jnp.int32, (1, SEL_KEYS), 1)
    place = jnp.where(lane < MID, lane - (MID - HALF), lane - (SEL_KEYS - HALF) + HALF)
    place = jnp.where((lane >= MID) & (lane < SEL_KEYS - HALF), -1, place)
    tall = lax.broadcasted_iota(jnp.int32, (SEL_KEYS, BLOCK), 0)
    fold = tall % HALF + jnp.where(tall >= MID, HALF, 0)
    fold = (fold == lax.broadcasted_iota(jnp.int32, (SEL_KEYS, BLOCK), 1)).astype(bf16)
    head = lax.broadcasted_iota(jnp.int32, (IDX_HEADS, 128), 0)
    wide_lane = lax.broadcasted_iota(jnp.int32, (IDX_HEADS, 128), 1)
    pairs = (
        lax.broadcasted_iota(jnp.int32, (32, IDX_HEADS), 1) // 2
        == lax.broadcasted_iota(jnp.int32, (32, IDX_HEADS), 0)
    ).astype(bf16)

    def choose(q):
        for k in range(SELECT):
            at = pl.multiple_of(apos[q * SELECT + k], 32)
            bt = pl.multiple_of(bpos[q * SELECT + k], 64)
            ropes = abuf[pl.ds(at + 128, HALF), :]
            for h in range(2):
                to = slice(h * MID + k * HALF, h * MID + (k + 1) * HALF)
                off = h * HALF
                ksel[q % 2, to, 0:128] = abuf[pl.ds(at + off, HALF), :]
                ksel[q % 2, to, 128:256] = abuf[pl.ds(at + 64 + off, HALF), :]
                ksel[q % 2, to, 256:384] = bbuf[pl.ds(bt + off, HALF), :]
                ksel[q % 2, to, 384:512] = bbuf[pl.ds(bt + 64 + off, HALF), :]
                if h:
                    ropes = jnp.concatenate([ropes[:, 64:], ropes[:, :64]], axis=1)
                ksel[q % 2, to, 512:640] = ropes
                isel[q % 2, to, :] = bbuf[pl.ds(bt + 128 + off, HALF), :]

    def score(q):
        scores[q % 2] = last(wide[q * HEADS : (q + 1) * HEADS, :], ksel[q % 2])

    choose(0)
    score(0)
    weights = jnp.zeros((32, 128), f32)
    for q in range(MINE):
        if q + 1 < MINE:
            choose(q + 1)
            score(q + 1)
        valid = place <= upto[q]
        target = jnp.zeros((8, SEL_KEYS), f32)
        for h in range(0, HEADS, 8):
            part = masked(scores[q % 2, h : h + 8, :], valid)
            high = jnp.max(part, axis=1, keepdims=True)
            raised = jnp.exp2((part - high) * (mla_scale * log2e))
            target = target + raised * (1.0 / jnp.sum(raised, axis=1, keepdims=True))
        target = jnp.sum(target, axis=0, keepdims=True) * (1.0 / HEADS)
        iq_rows = iq[q * IDX_HEADS : (q + 1) * IDX_HEADS, :]
        weight = wide_w[q * IDX_HEADS : (q + 1) * IDX_HEADS, :]
        affinities = last(iq_rows, isel[q % 2])
        logits = jnp.zeros((8, SEL_KEYS), f32)
        for h in range(0, IDX_HEADS, 8):
            affinity = affinities[h : h + 8] * inverse
            small = jnp.exp2(jnp.abs(affinity) * (-log2e))
            more = 1.0 + small
            soft = jnp.maximum(affinity, 0.0) + jnp.log(more)
            logits = logits + weight[h : h + 8, :1] * soft
            softs[h : h + 8, :] = soft
            gates[h : h + 8, :] = jnp.where(affinity >= 0.0, 1.0, small) / more
        logits = masked(jnp.sum(logits, axis=0, keepdims=True), valid)
        up = jnp.exp(logits - jnp.max(logits, axis=1, keepdims=True))
        chance = up * (1.0 / jnp.sum(up, axis=1, keepdims=True))
        grad_logit = jnp.where(valid, cot[q] * (chance - target), 0.0)
        grad_wide = grad_logit.astype(bf16).astype(f32)
        for h in range(0, IDX_HEADS, 16):
            slopes[h : h + 16, :] = (grad_wide * gates[h : h + 16, :]).astype(bf16)
        gq = jnp.dot(slopes[...], isel[q % 2], preferred_element_type=f32) * (weight * inverse)
        gw = jnp.sum(grad_wide * softs[...], axis=1, keepdims=True)
        outs[:, 2 * q : 2 * q + 2, :] = gq.reshape(32, 2, 128)
        gw = jnp.where(wide_lane == 2 * q + head % 2, gw, 0.0).astype(bf16)
        weights = weights + jnp.dot(pairs, gw, preferred_element_type=f32)
        spread = lax.broadcasted_iota(jnp.int32, (96, SEL_KEYS), 0) == place_of[q : q + 1, :]
        spread = jnp.where(spread, grad_wide, 0.0).astype(bf16)
        spread = jnp.dot(spread, fold, preferred_element_type=f32)
        outs[:, 8 + q : 9 + q, 0:64] = spread[0:32].reshape(32, 1, 64)
        outs[:, 8 + q : 9 + q, 64:128] = spread[32:64].reshape(32, 1, 64)
        half = slice(q % 2 * 64, q % 2 * 64 + 64)
        outs[:, 12 + q // 2 : 13 + q // 2, half] = spread[64:96].reshape(32, 1, 64)
    outs[:, 14:15, :] = weights.reshape(32, 1, 128)
    out[...] = outs[...].reshape(512, 128).astype(bf16)


def taken(got, row):
    query = lax.broadcasted_iota(jnp.int32, (128, 512), 0)
    pick = lax.broadcasted_iota(jnp.int32, (128, 512), 1) == query // MINE * 16 + row(query % MINE)
    return jnp.dot(pick.astype(bf16), got[...], preferred_element_type=f32)


def key_kernel(got, gates, turned, out):
    low = taken(got, lambda q: 8 + q)
    high = taken(got, lambda q: 12 + q // 2)
    odd = lax.broadcasted_iota(jnp.int32, (128, 1), 0) % 2 == 1
    grad = jnp.concatenate([low, jnp.where(odd, high[:, 64:], high[:, :64])], axis=1)
    total = jnp.zeros((128, 192), f32)
    for j in range(0, IDX_HEADS, 4):
        slopes = [
            (grad * gates[n * 128 : (n + 1) * 128, :].astype(f32)).astype(bf16)
            for n in range(j, j + 4)
        ]
        total = total + jnp.dot(
            turned[:, j * 128 : (j + 4) * 128],
            jnp.concatenate(slopes, axis=0),
            preferred_element_type=f32,
        )
    part = total.T.astype(bf16)
    for n in range(8):
        out[n * 192 : (n + 1) * 192, :] = part


def end_kernel(got, gq, gw):
    for h in range(2):
        gq[:, h * 128 : (h + 1) * 128] = taken(got, lambda q: 2 * q + h)
    rows = taken(got, lambda q: 14)
    query = lax.broadcasted_iota(jnp.int32, (128, 128), 0)
    lane = lax.broadcasted_iota(jnp.int32, (128, 128), 1)
    for h in range(2):
        one = jnp.where(lane == query % MINE * 2 + h, rows, 0.0)
        gw[:, h : h + 1] = jnp.sum(one, axis=1, keepdims=True)


def body(query_latent, kv_latent, index_query, index_key, head_weight, chosen, loss_grad):
    x, zl, core = lax.axis_index("x"), lax.axis_index("zl"), lax.axis_index("core")
    col = (x * 4 + zl) * 2 + core
    pieces, queries = gather_keys(index_key, kv_latent, query_latent.reshape(32, MINE, 4 * LATENT))
    queries = queries.reshape(32 * MINE, 4 * LATENT)
    wide = call(query_kernel, (queries,), struct((512, 640), bf16))
    first = col * MINE
    picked = lax.dynamic_slice_in_dim(chosen, first, MINE, 0)
    nblocks = picked.shape[1]
    before = jnp.tril(jnp.ones((nblocks, nblocks), jnp.int32), -1)
    rank = jnp.sum(picked[:, None, :] * before[None], axis=2)
    hit = (rank[:, :, None] == jnp.arange(SELECT)[None, None, :]) & (picked[:, :, None] > 0)
    block = jnp.sum(jnp.where(hit, jnp.arange(nblocks)[None, :, None], 0), axis=1).reshape(-1)
    owner, sub = block // 3, block % 3
    dx, dz, dc = (owner // 8 - x) % 4, (owner // 2 % 4 - zl) % 4, (owner + core) % 2
    apos = ((dc * 4 + dx) * 4 + dz) * A + sub * ROWS_A
    bpos = ((dc * 4 + dz) * 4 + dx) * B + sub * ROWS_B
    place = jnp.broadcast_to((sub * 32 + owner).reshape(MINE, SELECT, 1), (MINE, SELECT, HALF))
    place = place.reshape(MINE, MID)
    place = jnp.concatenate([place, place], axis=1)
    row = lax.axis_index("zh") * 4 + lax.axis_index("y")
    upto = (KEYS - 1024 + row * 128 + first + jnp.arange(MINE)) % BLOCK
    cot = lax.dynamic_slice_in_dim(loss_grad, first, MINE, 0)
    iq = lax.dynamic_slice_in_dim(index_query, first, MINE, 0).reshape(MINE * IDX_HEADS, IDX_DIM)
    weight = lax.dynamic_slice_in_dim(head_weight, first, MINE, 0).reshape(MINE * IDX_HEADS, 1)
    weight = jnp.broadcast_to(weight, (MINE * IDX_HEADS, 128))
    gates, turned = call(
        gate_kernel,
        (index_query, index_key, head_weight),
        (struct((8192, 192), bf16), struct((128, 8192), bf16)),
        flops=2 * 8192 * 192 * 128,
        nbytes=8 << 20,
    )
    small = (apos, bpos, upto, cot, wide, iq, weight, place, gates, turned)
    pieces[2], small = lax.optimization_barrier((pieces[2], small))
    gates, turned = small[8:]
    other = [shift(piece, "core", 2, 1) for piece in pieces]
    pieces = pieces[:4] + other[:4] + pieces[4:] + other[4:]
    out = call(
        kernel,
        (*small[:8], *pieces),
        struct((512, 128), bf16),
        flops=2 * MINE * SEL_KEYS * (HEADS * LATENT + 2 * IDX_HEADS * IDX_DIM),
        nbytes=KEYS * 704 * 2,
        scratch=[
            pltpu.VMEM((32 * A, 128), bf16),
            pltpu.VMEM((32 * B, 128), bf16),
            pltpu.VMEM((2, SEL_KEYS, 640), bf16),
            pltpu.VMEM((2, SEL_KEYS, 128), bf16),
            pltpu.VMEM((2, HEADS, SEL_KEYS), f32),
            pltpu.VMEM((IDX_HEADS, SEL_KEYS), f32),
            pltpu.VMEM((IDX_HEADS, SEL_KEYS), f32),
            pltpu.VMEM((IDX_HEADS, SEL_KEYS), bf16),
            pltpu.VMEM((32, 16, 128), f32),
            pltpu.SemaphoreType.DMA((16,)),
        ],
        specs=[SMEM] * 4 + [VMEM] * 4 + [ANY] * 16,
    )
    got = lax.all_to_all(out, COL, 0, 0, tiled=True)
    part = call(
        key_kernel,
        (got, gates, turned),
        struct((8 * 192, 128), bf16),
        flops=2 * 8192 * 192 * 128,
        nbytes=8 << 20,
    )
    parts = lax.all_to_all(part, ("zh", "y"), 0, 0, tiled=True)
    grad_key = jnp.sum(parts.reshape(8, 192, 128).astype(f32), axis=0) * inverse
    gq, gw = call(end_kernel, (got,), (struct((128, 256), f32), struct((128, 2), f32)))
    return gq, grad_key, gw


def solution(mesh):
    wide = Mesh(mesh.devices.reshape(2, 4, 4, 4, 2), ("zh", "y", "x", "zl", "core"))
    row = ("zh", "y")
    in_specs = (
        P(row, COL),
        P(COL, None),
        P(row, None),
        P(COL, None),
        P(row, None),
        P(row, None),
        P(row),
    )
    out_specs = (P(row, COL), P(COL, None), P(row, COL))
    return jax.shard_map(body, mesh=wide, in_specs=in_specs, out_specs=out_specs, check_vma=False)
```

```python
import jax
import jax.numpy as jnp
from jax import lax
from jax.experimental import pallas as pl
from jax.experimental.pallas import tpu as pltpu
from jax.sharding import Mesh, PartitionSpec as P

LATENT = 576
IDX_DIM = 128
IDX_HEADS = 64
HEADS = 128
BLOCK = 64
HALF = BLOCK // 2
SELECT = 32
MINE = 4
KEYS = 6144
SEL_KEYS = SELECT * BLOCK
MID = SEL_KEYS // 2
ROWS_A = 160
ROWS_B = 192
A, B = 3 * ROWS_A, 3 * ROWS_B
mla_scale = 192.0 ** (-0.5)
inverse = IDX_DIM ** (-0.5)
log2e = 1.4426950408889634
big_negative = -1e30
COL = ("x", "zl", "core")
Z = ("zh", "zl")
bf16, f32 = jnp.bfloat16, jnp.float32
SMEM = pl.BlockSpec(memory_space=pltpu.SMEM)
VMEM = pl.BlockSpec(memory_space=pltpu.VMEM)
ANY = pl.BlockSpec(memory_space=pl.ANY)


def struct(shape, dtype):
    return jax.ShapeDtypeStruct(shape, dtype)


def call(kernel, ins, out_shape, flops=0, nbytes=1 << 20, scratch=(), specs=None, mib=12):
    return pl.pallas_call(
        kernel,
        out_shape=out_shape,
        in_specs=specs or [VMEM] * len(ins),
        out_specs=jax.tree.map(lambda _: VMEM, out_shape),
        scratch_shapes=scratch,
        cost_estimate=pl.CostEstimate(flops=flops, bytes_accessed=nbytes, transcendentals=0),
        compiler_params=pltpu.CompilerParams(vmem_limit_bytes=mib << 20),
    )(*ins)


def shift(value, axis, size, by):
    return lax.ppermute(value, axis, [(i, (i + by) % size) for i in range(size)])


def around_z(value):
    two = [(2 * z + c, 2 * ((z + (2, -2)[c]) % 8) + c) for z in range(8) for c in range(2)]
    return [
        shift(value, Z, 8, -1),
        lax.ppermute(value, ("zh", "zl", "core"), two),
        shift(value, Z, 8, 1),
    ]


def around_x(value):
    return [shift(value, "x", 4, -1), shift(value, "x", 4, 2), shift(value, "x", 4, 1)]


def pack_kernel(ik, kv, a, b):
    for s in range(3):
        at = slice(s * BLOCK, (s + 1) * BLOCK)
        low, high = s * BLOCK, s * BLOCK + HALF
        a[s * ROWS_A : s * ROWS_A + 64, :] = kv[at, 0:128]
        a[s * ROWS_A + 64 : s * ROWS_A + 128, :] = kv[at, 128:256]
        a[s * ROWS_A + 128 : (s + 1) * ROWS_A, :] = jnp.concatenate(
            [kv[low:high, 512:576], kv[high : high + HALF, 512:576]], axis=1
        )
        b[s * ROWS_B : s * ROWS_B + 64, :] = kv[at, 256:384]
        b[s * ROWS_B + 64 : s * ROWS_B + 128, :] = kv[at, 384:512]
        b[s * ROWS_B + 128 : (s + 1) * ROWS_B, :] = ik[at, :]


def join_kernel(*refs):
    for n in range(8):
        rows = refs[n].shape[0]
        refs[8 + n // 4][n % 4 * rows : (n % 4 + 1) * rows, :] = refs[n][...]


def join(first, second):
    out = (struct((4 * A, 128), bf16), struct((4 * B, 128), bf16))
    return call(join_kernel, first + second, out)


def gather_keys(index_key, kv_latent, query_latent):
    a, b = call(
        pack_kernel, (index_key, kv_latent), (struct((A, 128), bf16), struct((B, 128), bf16))
    )
    near_z, near_x = around_z(a), around_x(b)
    near_z, near_x = lax.optimization_barrier((near_z, near_x))
    ua, ub = join([a] + near_z, [b] + near_x)
    queries = lax.all_to_all(query_latent, COL, 0, 0, tiled=True)
    return [ua] + around_x(ua) + [ub] + around_z(ub), queries


def last(a, b):
    return lax.dot_general(a, b, (((1,), (1,)), ((), ())), preferred_element_type=f32)


def query_kernel(queries, wide):
    zero = jnp.zeros((HEADS, 64), bf16)
    for q in range(MINE):
        pick = (
            lax.broadcasted_iota(jnp.int32, (32, 128), 1)
            == lax.broadcasted_iota(jnp.int32, (32, 128), 0) * MINE + q
        )
        rows = jnp.dot(pick.astype(bf16), queries[...], preferred_element_type=f32).astype(bf16)
        heads = jnp.concatenate([rows[:, h * LATENT : (h + 1) * LATENT] for h in range(4)], axis=0)
        wide[q * HEADS : (q + 1) * HEADS, :] = jnp.concatenate([heads, zero], axis=1)


def masked(values, valid):
    one, two = slice(MID - 128, MID), slice(SEL_KEYS - 128, SEL_KEYS)
    return jnp.concatenate(
        [
            values[:, : MID - 128],
            jnp.where(valid[:, one], values[:, one], big_negative),
            values[:, MID : SEL_KEYS - 128],
            jnp.where(valid[:, two], values[:, two], big_negative),
        ],
        axis=1,
    )


def gate_kernel(index_query, index_key, head_weight, gates, weighted):
    lane = lax.broadcasted_iota(jnp.int32, head_weight.shape, 1)

    @pl.loop(0, IDX_HEADS // 4)
    def _(n):
        for m in range(4):
            j = n * 4 + m
            rows = pl.ds(pl.multiple_of(j * 128, 128), 128)
            iq = index_query[:, rows]
            affinity = last(index_key[...], iq)
            gates[:, rows] = (jnp.tanh(affinity * (0.5 * inverse)) * 0.5 + 0.5).astype(bf16)
            weight = jnp.sum(jnp.where(lane == j, head_weight[...], 0.0), axis=1, keepdims=True)
            weighted[rows, :] = (weight * iq.astype(f32)).astype(bf16)


def kernel(apos, bpos, upto, cot, *rest):
    pieces = rest[4:20]
    out = rest[20]
    abuf, bbuf, ksel, isel, scores, softs, gates, slopes, outs = rest[21:30]
    wide, iq, wide_w, place_of, sems = rest[30:]
    copies = [
        pltpu.make_async_copy(rest[n], (wide, iq, wide_w, place_of)[n], sems.at[16 + n])
        for n in range(4)
    ]
    for n in range(16):
        buf, rows = (abuf, 4 * A) if n < 8 else (bbuf, 4 * B)
        copies.append(
            pltpu.make_async_copy(pieces[n], buf.at[pl.ds(n % 8 * rows, rows)], sems.at[n])
        )
    for copy in copies:
        copy.start()
    outs[...] = jnp.zeros_like(outs)
    for copy in copies:
        copy.wait()
    lane = lax.broadcasted_iota(jnp.int32, (1, SEL_KEYS), 1)
    place = jnp.where(lane < MID, lane - (MID - HALF), lane - (SEL_KEYS - HALF) + HALF)
    place = jnp.where((lane >= MID) & (lane < SEL_KEYS - HALF), -1, place)
    tall = lax.broadcasted_iota(jnp.int32, (SEL_KEYS, BLOCK), 0)
    fold = tall % HALF + jnp.where(tall >= MID, HALF, 0)
    fold = (fold == lax.broadcasted_iota(jnp.int32, (SEL_KEYS, BLOCK), 1)).astype(bf16)
    blocks = lax.broadcasted_iota(jnp.int32, (SELECT, SEL_KEYS), 1) % MID // HALF
    blocks = blocks == lax.broadcasted_iota(jnp.int32, (SELECT, SEL_KEYS), 0)
    head = lax.broadcasted_iota(jnp.int32, (IDX_HEADS, 128), 0)
    wide_lane = lax.broadcasted_iota(jnp.int32, (IDX_HEADS, 128), 1)
    pairs = (
        lax.broadcasted_iota(jnp.int32, (32, IDX_HEADS), 1) // 2
        == lax.broadcasted_iota(jnp.int32, (32, IDX_HEADS), 0)
    ).astype(bf16)

    def choose_index(q):
        for k in range(SELECT):
            bt = pl.multiple_of(bpos[q * SELECT + k], 64)
            for h in range(2):
                to = slice(h * MID + k * HALF, h * MID + (k + 1) * HALF)
                isel[q % 2, to, :] = bbuf[pl.ds(bt + 128 + h * HALF, HALF), :]

    def choose(q, k):
        at = pl.multiple_of(apos[q * SELECT + k], 32)
        bt = pl.multiple_of(bpos[q * SELECT + k], 64)
        ropes = abuf[pl.ds(at + 128, HALF), :]
        for h in range(2):
            to = slice(h * MID + k * HALF, h * MID + (k + 1) * HALF)
            off = h * HALF
            ksel[q % 2, to, 0:128] = abuf[pl.ds(at + off, HALF), :]
            ksel[q % 2, to, 128:256] = abuf[pl.ds(at + 64 + off, HALF), :]
            ksel[q % 2, to, 256:384] = bbuf[pl.ds(bt + off, HALF), :]
            ksel[q % 2, to, 384:512] = bbuf[pl.ds(bt + 64 + off, HALF), :]
            if h:
                ropes = jnp.concatenate([ropes[:, 64:], ropes[:, :64]], axis=1)
            ksel[q % 2, to, 512:640] = ropes
        if k % 8 == 7:
            for start in ((k - 7) * HALF, MID + (k - 7) * HALF):
                to = slice(start, start + 256)
                scores[q % 2, :, to] = last(
                    wide[q * HEADS : (q + 1) * HEADS, :], ksel[q % 2, to, :]
                )

    ahead = [(0, k) for k in range(SELECT)]

    def advance(count):
        for _ in range(count):
            if ahead:
                choose(*ahead.pop(0))

    choose_index(0)
    weights = jnp.zeros((32, 128), f32)
    for q in range(MINE):
        valid = place <= upto[q]
        if 0 < q < MINE - 1:
            ahead.extend((q + 1, k) for k in range(SELECT))
        iq_rows = iq[q * IDX_HEADS : (q + 1) * IDX_HEADS, :]
        weight = wide_w[q * IDX_HEADS : (q + 1) * IDX_HEADS, :]
        affinities = last(iq_rows, isel[q % 2])
        logits = jnp.zeros((8, SEL_KEYS), f32)
        for h in range(0, IDX_HEADS, 8):
            advance(4 if q == 0 else 2)
            affinity = affinities[h : h + 8] * inverse
            small = jnp.exp2(jnp.abs(affinity) * (-log2e))
            soft = jnp.maximum(affinity, 0.0) + jnp.log(1.0 + small)
            logits = logits + weight[h : h + 8, :1] * soft
            softs[h : h + 8, :] = soft
            gates[h : h + 8, :] = jnp.tanh(affinity * 0.5) * 0.5 + 0.5
        if q + 1 < MINE:
            choose_index(q + 1)
            if q == 0:
                ahead.extend((1, k) for k in range(SELECT))
        target = jnp.zeros((8, SEL_KEYS), f32)
        for h in range(0, HEADS, 8):
            advance(2 if q == 0 else 1)
            part = masked(scores[q % 2, h : h + 8, :], valid)
            high = jnp.max(part, axis=1, keepdims=True)
            raised = jnp.exp2((part - high) * (mla_scale * log2e))
            target = target + raised * (1.0 / jnp.sum(raised, axis=1, keepdims=True))
        target = jnp.sum(target, axis=0, keepdims=True) * (1.0 / HEADS)
        logits = masked(jnp.sum(logits, axis=0, keepdims=True), valid)
        up = jnp.exp(logits - jnp.max(logits, axis=1, keepdims=True))
        chance = up * (1.0 / jnp.sum(up, axis=1, keepdims=True))
        grad_logit = jnp.where(valid, cot[q] * (chance - target), 0.0)
        grad_wide = grad_logit.astype(bf16).astype(f32)
        for h in range(0, IDX_HEADS, 16):
            slopes[h : h + 16, :] = (grad_wide * gates[h : h + 16, :]).astype(bf16)
        gq = jnp.dot(slopes[...], isel[q % 2], preferred_element_type=f32) * (weight * inverse)
        gw = jnp.sum(grad_wide * softs[...], axis=1, keepdims=True)
        outs[:, 2 * q : 2 * q + 2, :] = gq.reshape(32, 2, 128)
        gw = jnp.where(wide_lane == 2 * q + head % 2, gw, 0.0).astype(bf16)
        weights = weights + jnp.dot(pairs, gw, preferred_element_type=f32)
        spread = jnp.where(blocks, grad_wide, 0.0).astype(bf16)
        spread = jnp.dot(spread, fold, preferred_element_type=f32).astype(bf16)
        where_to = lax.broadcasted_iota(jnp.int32, (96, 32), 0) == place_of[q : q + 1, :32]
        spread = jnp.dot(where_to.astype(bf16), spread, preferred_element_type=f32)
        outs[:, 8 + q : 9 + q, 0:64] = spread[0:32].reshape(32, 1, 64)
        outs[:, 8 + q : 9 + q, 64:128] = spread[32:64].reshape(32, 1, 64)
        half = slice(q % 2 * 64, q % 2 * 64 + 64)
        outs[:, 12 + q // 2 : 13 + q // 2, half] = spread[64:96].reshape(32, 1, 64)
    outs[:, 14:15, :] = weights.reshape(32, 1, 128)
    out[...] = outs[...].reshape(512, 128).astype(bf16)


def taken(got, row):
    query = lax.broadcasted_iota(jnp.int32, (128, 512), 0)
    pick = lax.broadcasted_iota(jnp.int32, (128, 512), 1) == query // MINE * 16 + row(query % MINE)
    return jnp.dot(pick.astype(bf16), got[...], preferred_element_type=f32)


def key_kernel(got, gates, weighted, out):
    low = taken(got, lambda q: 8 + q)
    high = taken(got, lambda q: 12 + q // 2)
    odd = lax.broadcasted_iota(jnp.int32, (128, 1), 0) % 2 == 1
    high = jnp.where(odd, high[:, 64:], high[:, :64])
    grad = jnp.concatenate([low.T, high.T], axis=0).astype(bf16)
    total = jnp.zeros((192, 128), f32)
    for j in range(0, IDX_HEADS, 4):
        rows = slice(j * 128, (j + 4) * 128)
        slopes = jnp.concatenate([grad] * 4, axis=1) * gates[:, rows]
        total = total + jnp.dot(slopes, weighted[rows, :], preferred_element_type=f32)
    out[...] = total.astype(bf16)


def end_kernel(got, gq, gw):
    for h in range(2):
        gq[:, h * 128 : (h + 1) * 128] = taken(got, lambda q: 2 * q + h)
    rows = taken(got, lambda q: 14)
    query = lax.broadcasted_iota(jnp.int32, (128, 128), 0)
    lane = lax.broadcasted_iota(jnp.int32, (128, 128), 1)
    for h in range(2):
        one = jnp.where(lane == query % MINE * 2 + h, rows, 0.0)
        gw[:, h : h + 1] = jnp.sum(one, axis=1, keepdims=True)


def body(query_latent, kv_latent, index_query, index_key, head_weight, chosen, loss_grad):
    x, zl, core = lax.axis_index("x"), lax.axis_index("zl"), lax.axis_index("core")
    col = (x * 4 + zl) * 2 + core
    pieces, queries = gather_keys(index_key, kv_latent, query_latent.reshape(32, MINE, 4 * LATENT))
    queries = queries.reshape(32 * MINE, 4 * LATENT)
    wide = call(query_kernel, (queries,), struct((512, 640), bf16))
    first = col * MINE
    picked = lax.dynamic_slice_in_dim(chosen, first, MINE, 0)
    nblocks = picked.shape[1]
    before = jnp.tril(jnp.ones((nblocks, nblocks), jnp.int32), -1)
    rank = jnp.sum(picked[:, None, :] * before[None], axis=2)
    hit = (rank[:, :, None] == jnp.arange(SELECT)[None, None, :]) & (picked[:, :, None] > 0)
    block = jnp.sum(jnp.where(hit, jnp.arange(nblocks)[None, :, None], 0), axis=1).reshape(-1)
    owner, sub = block // 3, block % 3
    dx, dz, dc = (owner // 8 - x) % 4, (owner // 2 % 4 - zl) % 4, (owner + core) % 2
    apos = ((dc * 4 + dx) * 4 + dz) * A + sub * ROWS_A
    bpos = ((dc * 4 + dz) * 4 + dx) * B + sub * ROWS_B
    place = jnp.pad((sub * 32 + owner).reshape(MINE, SELECT), ((0, 0), (0, 96)))
    row = lax.axis_index("zh") * 4 + lax.axis_index("y")
    upto = (KEYS - 1024 + row * 128 + first + jnp.arange(MINE)) % BLOCK
    cot = lax.dynamic_slice_in_dim(loss_grad, first, MINE, 0)
    iq = lax.dynamic_slice_in_dim(index_query, first, MINE, 0).reshape(MINE * IDX_HEADS, IDX_DIM)
    weight = lax.dynamic_slice_in_dim(head_weight, first, MINE, 0).reshape(MINE * IDX_HEADS, 1)
    weight = jnp.broadcast_to(weight, (MINE * IDX_HEADS, 128))
    beside = shift(pieces[0], "core", 2, 1)
    beside, late_query = lax.optimization_barrier((beside, index_query))
    gates, turned = call(
        gate_kernel,
        (late_query, index_key, head_weight),
        (struct((192, 8192), bf16), struct((8192, 128), bf16)),
        flops=2 * 8192 * 192 * 128,
        nbytes=8 << 20,
    )
    small = (apos, bpos, upto, cot, wide, iq, weight, place, gates, turned)
    pieces[2], pieces[6], small = lax.optimization_barrier((pieces[2], pieces[6], small))
    gates, turned = small[8:]
    other = [beside] + [shift(piece, "core", 2, 1) for piece in pieces[1:]]
    pieces = pieces[:4] + other[:4] + pieces[4:] + other[4:]
    out = call(
        kernel,
        (*small[:8], *pieces),
        struct((512, 128), bf16),
        flops=2 * MINE * SEL_KEYS * (HEADS * LATENT + 2 * IDX_HEADS * IDX_DIM),
        nbytes=KEYS * 704 * 2,
        scratch=[
            pltpu.VMEM((32 * A, 128), bf16),
            pltpu.VMEM((32 * B, 128), bf16),
            pltpu.VMEM((2, SEL_KEYS, 640), bf16),
            pltpu.VMEM((2, SEL_KEYS, 128), bf16),
            pltpu.VMEM((2, HEADS, SEL_KEYS), f32),
            pltpu.VMEM((IDX_HEADS, SEL_KEYS), f32),
            pltpu.VMEM((IDX_HEADS, SEL_KEYS), f32),
            pltpu.VMEM((IDX_HEADS, SEL_KEYS), bf16),
            pltpu.VMEM((32, 16, 128), f32),
            pltpu.VMEM((MINE * HEADS, 640), bf16),
            pltpu.VMEM((MINE * IDX_HEADS, IDX_DIM), bf16),
            pltpu.VMEM((MINE * IDX_HEADS, 128), f32),
            pltpu.VMEM((MINE, 128), jnp.int32),
            pltpu.SemaphoreType.DMA((20,)),
        ],
        specs=[SMEM] * 4 + [ANY] * 20,
        mib=32,
    )
    got = lax.all_to_all(out, COL, 0, 0, tiled=True)
    part = call(
        key_kernel,
        (got, gates, turned),
        struct((192, 128), bf16),
        flops=2 * 8192 * 192 * 128,
        nbytes=8 << 20,
    )
    gq, gw = call(end_kernel, (got,), (struct((128, 256), f32), struct((128, 2), f32)))
    opposite, gq, gw = lax.optimization_barrier((shift(part, "zh", 2, 1), gq, gw))
    part = part.astype(f32) + opposite.astype(f32)
    part = (part + shift(part, "y", 4, 2)) + (shift(part, "y", 4, 1) + shift(part, "y", 4, -1))
    grad_key = part * inverse
    return gq, grad_key, gw


def solution(mesh):
    wide = Mesh(mesh.devices.reshape(2, 4, 4, 4, 2), ("zh", "y", "x", "zl", "core"))
    row = ("zh", "y")
    in_specs = (
        P(row, COL),
        P(COL, None),
        P(row, None),
        P(COL, None),
        P(row, None),
        P(row, None),
        P(row),
    )
    out_specs = (P(row, COL), P(COL, None), P(row, COL))
    return jax.shard_map(body, mesh=wide, in_specs=in_specs, out_specs=out_specs, check_vma=False)
```
